256 devices in a mesh: blk: 128 (over x, y, z), ch: 2 (over core).
Axes of the slice: x: 4, y: 4, z: 8, core: 2. Of those that a mesh axis runs over, the one named last changes fastest.
Arguments:
- features: bfloat16 [32768, 128], P('blk'), may hold values from -6 to 6
- out_grad: bfloat16 [32768, 256], P('blk', 'ch'), may hold values from -6 to 6
- weight: bfloat16 [256, 256], P('ch'), may hold values from -0.375 to 0.375
- neighbour_slot: int32 [32768, 20], P('blk'), may hold values from 0 to 2303
- argmax_edge: int32 [32768, 256], P('blk', 'ch'), may hold values from 0 to 19
Outputs:
- feature_grad: float32 [32768, 128], P('blk')
- weight_grad: float32 [256, 256], P('ch')
The draws below stay inside these ranges and needn't reach their ends.
Inputs may be any that keep to these rules, and one draw needn't show every extreme that they name: `neighbour_slot`: slot s stands for row s mod 256 of the block s // 256 - 4 places away from the point's own block around the cycle.
All inputs are finite; a program needn't handle non-finite values.
Results may differ from the reference program's by a relative error of at most 0.0044.
Values may be sent and summed in bfloat16 or wider, within the bound.
A program may use at most 64 MiB of HBM per device.

```python
import jax
import jax.numpy as jnp
from jax import lax

CIN = 128
COUT = 256
KNN = 20
REACH = 4
PTS = 256
POINTS = 32768
N_BLK = 128


def plant(drawn, key, low, largest):
    longest = drawn.shape.index(max(drawn.shape))
    spots = []
    for shift in (0, 1):
        where = [jax.random.randint(jax.random.fold_in(key, axis), (), 0, length) for axis, length in enumerate(drawn.shape)]
        where[longest] = (where[longest] + shift) % drawn.shape[longest]
        spots.append(tuple(where))
    return drawn.at[spots[0]].set(low).at[spots[1]].set(largest)


def steps_of(stream_key, dims, cuts, low, high):
    factor_of = 1.0
    for axis_at, blocks in cuts:
        draws = jax.random.uniform(jax.random.fold_in(jax.random.fold_in(stream_key, 6), axis_at), (blocks,), jnp.float32, low / len(cuts), high / len(cuts))
        factor_of = factor_of * jnp.repeat(jnp.exp(draws), dims[axis_at] // blocks).reshape((-1,) + (1,) * (len(dims) - 1 - axis_at))
    return factor_of


def noise(own_key, shape, width, bound, shards=(), kind=jnp.bfloat16):
    level = steps_of(own_key, shape, shards, -0.22, 0.18) if shards else 1.0
    result = jax.random.normal(own_key, shape, jnp.float32) * width * level
    return jnp.minimum(jnp.maximum(result, -bound), bound).astype(kind)


def setup_inputs(seed: int = 0) -> dict:
    keys = jax.random.split(jax.random.key(seed), 6)
    features = noise(keys[0], (POINTS, CIN), 1.0, 6.0, ((0, 128),))
    out_grad = noise(keys[1], (POINTS, COUT), 1.0, 6.0, ((0, 128), (1, 2)))
    weight = noise(keys[2], (COUT, 2 * CIN), (2 * CIN) ** -0.5, 0.375, ((0, 2),))
    neighbour_slot = plant(jax.random.randint(keys[3], (POINTS, KNN), 0, (2 * REACH + 1) * PTS), jax.random.fold_in(keys[3], 1), 0, ((2 * REACH + 1) * PTS) - 1).astype(jnp.int32)
    argmax_edge = plant(jax.random.randint(keys[4], (POINTS, COUT), 0, KNN), jax.random.fold_in(keys[4], 1), 0, KNN - 1).astype(jnp.int32)
    return dict(features=features, out_grad=out_grad, weight=weight, neighbour_slot=neighbour_slot, argmax_edge=argmax_edge)


def silu_slope(pre):
    sig = jax.nn.sigmoid(pre)
    return sig * (1.0 + pre * (1.0 - sig))


def reference(features, out_grad, weight, neighbour_slot, argmax_edge):
    in_width = features.shape[1]
    w_self = weight[:, :in_width]
    w_nbr = weight[:, in_width:]
    w_diff = (w_self.astype(jnp.float32) - w_nbr.astype(jnp.float32)).astype(jnp.bfloat16)
    offsets = jnp.arange(2 * REACH + 1, dtype=jnp.int32) - REACH
    row_ids = jnp.arange(PTS, dtype=jnp.int32)
    edge_ids = jnp.arange(KNN, dtype=jnp.int32)
    window_rows = (2 * REACH + 1) * PTS

    def per_block(running, block_id):
        grad_acc, weight_acc = running
        owners = (block_id + offsets) % N_BLK
        rows = (owners[:, None] * PTS + row_ids[None, :]).reshape(-1).astype(jnp.int32)
        window = features[rows]
        start = (block_id * PTS).astype(jnp.int32)
        own_rows = lax.dynamic_slice_in_dim(features, start, PTS, 0)
        own_grad = lax.dynamic_slice_in_dim(out_grad, start, PTS, 0)
        slots = lax.dynamic_slice_in_dim(neighbour_slot, start, PTS, 0)
        picks = lax.dynamic_slice_in_dim(argmax_edge, start, PTS, 0)
        self_term = jnp.dot(own_rows, w_diff.T, preferred_element_type=jnp.float32)
        values = jnp.dot(window, w_nbr.T, preferred_element_type=jnp.float32)
        pre = self_term[:, None, :] + values[slots]
        keep = picks[:, None, :] == edge_ids[None, :, None]
        edge_grad = jnp.where(keep, own_grad.astype(jnp.float32)[:, None, :] * silu_slope(pre), 0.0).astype(jnp.bfloat16)
        grad_sum = jnp.sum(edge_grad.astype(jnp.float32), axis=1).astype(jnp.bfloat16)
        gathered = jax.ops.segment_sum(edge_grad.reshape(-1, edge_grad.shape[2]).astype(jnp.float32), slots.reshape(-1), num_segments=window_rows).astype(jnp.bfloat16)
        contrib = jnp.dot(gathered, w_nbr, preferred_element_type=jnp.float32)
        self_grad = jnp.dot(grad_sum, w_diff, preferred_element_type=jnp.float32)
        contrib = contrib.at[REACH * PTS:(REACH + 1) * PTS].add(self_grad)
        grad_acc = grad_acc.at[rows].add(contrib)
        own_part = lax.dot_general(grad_sum, own_rows, (((0,), (0,)), ((), ())), preferred_element_type=jnp.float32)
        nbr_total = lax.dot_general(gathered, window, (((0,), (0,)), ((), ())), preferred_element_type=jnp.float32)
        weight_acc = weight_acc + jnp.concatenate([own_part, nbr_total - own_part], axis=1)
        return (grad_acc, weight_acc), None

    start_state = (jnp.zeros((POINTS, in_width), jnp.float32), jnp.zeros(weight.shape, jnp.float32))
    (grad_acc, weight_acc), _ = lax.scan(per_block, start_state, jnp.arange(N_BLK, dtype=jnp.int32))
    return grad_acc, weight_acc * (POINTS ** -0.5)
```

```python
import jax
import jax.numpy as jnp
from jax import lax
from jax.experimental import pallas as pl
from jax.experimental.pallas import tpu as pltpu
from jax.sharding import PartitionSpec as P

REACH = 4
SPAN = 2 * REACH + 1
NB = 128
PTS = 256
HALF = 128
CIN = 128
KNN = 20
MESH = pl.DeviceIdType.MESH
F32, BF16, I32 = jnp.float32, jnp.bfloat16, jnp.int32
NT = (((1,), (1,)), ((), ()))
TN = (((0,), (0,)), ((), ()))
FAR = (4, -4, 3, -3, 2, -2, 1, -1)
XY = sorted(
    [(dx, dy) for dx in range(4) for dy in range(4) if dx or dy],
    key=lambda t: -(min(t[0], 4 - t[0]) + min(t[1], 4 - t[1])),
)
ZO = (4, 3, 5, 2, 6, 1, 7)


def silu_slope(pre):
    sig = jax.nn.sigmoid(pre)
    return sig * (1.0 + pre * (1.0 - sig))


def kernel(
    f_hbm, g_hbm, w_hbm, s_hbm, a_hbm, fg_hbm, wg_hbm,
    win, gv, wv, sv, av, spad, s_t, low_t, grp_t, onehot, edges, pre, acc,
    part_out, part_in, mine, summed, got, fgv, wgv, rs_in, z_in, piece, wgo,
    in_sem, far_s, far_r, half_s, half_r, pp_s, pp_r, c_s, c_r,
    a1s, a1r, a2s, a2r, a3s, a3r, fo_s, fo_r, out_sem,
):
    b = lax.axis_index("blk")
    c = lax.axis_index("ch")
    partner = (b, 1 - c)
    line, z = b // 8, b % 8
    x, y = line // 4, line % 4
    far = [(lax.rem(b + k + NB, NB), c) for k in FAR]
    plane_at = [lax.rem(x + dx, 4) * 4 + lax.rem(y + dy, 4) for dx, dy in XY]
    plane = [(q * 8 + z, c) for q in plane_at]
    zline = [(line * 8 + lax.rem(z + dz, 8), c) for dz in ZO]

    bar = pltpu.get_barrier_semaphore()
    peers = far + [partner] + zline + plane
    for d in peers:
        pl.semaphore_signal(bar, inc=1, device_id=d, device_id_type=MESH)
    loads = [
        pltpu.make_async_copy(f_hbm, win.at[REACH], in_sem.at[0]),
        pltpu.make_async_copy(s_hbm, sv, in_sem.at[1]),
        pltpu.make_async_copy(a_hbm, av, in_sem.at[2]),
        pltpu.make_async_copy(w_hbm, wv, in_sem.at[3]),
        pltpu.make_async_copy(g_hbm, gv, in_sem.at[4]),
    ]
    for cp in loads:
        cp.start()
    loads[0].wait()
    pl.semaphore_wait(bar, len(peers))

    my_rows = pl.ds(pl.multiple_of(c * HALF, HALF), HALF)
    its_rows = pl.ds(pl.multiple_of((1 - c) * HALF, HALF), HALF)

    def rcopy(src, dst, ss, rs, dev):
        return pltpu.make_async_remote_copy(
            src_ref=src, dst_ref=dst, send_sem=ss, recv_sem=rs, device_id=dev, device_id_type=MESH
        )

    far_cp = []
    for k, d in zip(FAR, far):
        w = REACH - k
        cp = rcopy(win.at[REACH, my_rows], win.at[w, my_rows], far_s.at[w], far_r.at[w], d)
        cp.start()
        far_cp.append(cp)

    for cp in loads[1:]:
        cp.wait()
    spad[...] = jnp.zeros_like(spad)
    spad[:, :KNN] = sv[...]
    idx = jnp.take_along_axis(spad[...], av[...], axis=1, mode="promise_in_bounds")
    idx_t = idx.T
    low_t[...] = idx_t & 127
    grp_t[...] = idx_t >> 7
    s_t[...] = spad[...].T
    w_nbr = wv[:, CIN:]
    w_diff = (wv[:, :CIN].astype(F32) - w_nbr.astype(F32)).astype(BF16)
    row_ids = lax.broadcasted_iota(I32, (HALF, PTS), 0).astype(F32).astype(BF16)

    @pl.loop(0, KNN)
    def _(k):
        row = s_t[pl.ds(k, 1), :]
        low = (row & 127).astype(F32)
        blk = row >> 8
        cols = pl.ds(pl.multiple_of(k * PTS, PTS), PTS)
        for w in range(SPAN):
            key = jnp.broadcast_to(jnp.where(blk == w, low, -1.0), (HALF, PTS)).astype(BF16)
            onehot[w * HALF : (w + 1) * HALF, cols] = jnp.where(row_ids == key, 1.0, 0.0).astype(BF16)

    pre[...] = lax.dot_general(w_diff, win[REACH], NT, preferred_element_type=F32)

    def pick(w):
        vals = lax.dot_general(w_nbr, win[w], NT, preferred_element_type=F32)
        for h in range(2):
            cols = slice(h * HALF, (h + 1) * HALF)
            low, grp, p = low_t[:, cols], grp_t[:, cols], pre[:, cols]
            for g in range(2):
                table = vals[:, g * HALF : (g + 1) * HALF]
                hit = jnp.take_along_axis(table, low, axis=1, mode="promise_in_bounds")
                p = jnp.where(grp == 2 * w + g, p + hit, p)
            pre[:, cols] = p

    pick(REACH)
    half_cp = {}
    last = None
    for k in FAR + (None,):
        if k is not None:
            w = REACH - k
            rcopy(win.at[w, my_rows], win.at[w, my_rows], far_s.at[w], far_r.at[w], partner).wait_recv()
            half_cp[w] = rcopy(win.at[w, my_rows], win.at[w, my_rows], half_s.at[w], half_r.at[w], partner)
            half_cp[w].start()
        if last is not None:
            rcopy(win.at[last, my_rows], win.at[last, its_rows], half_s.at[last], half_r.at[last], partner).wait_recv()
            pick(last)
        last = None if k is None else w

    edge = (gv[...].astype(F32) * silu_slope(pre[...].T)).astype(BF16)
    upper = (idx >> 7) & 1
    ef, af = edge.astype(F32), av[...].astype(F32)
    e2 = jnp.concatenate([jnp.where(upper == 0, ef, 0.0), jnp.where(upper == 1, ef, 0.0)], axis=1).astype(BF16)
    a2 = jnp.concatenate([jnp.where(upper == 0, af, -1.0), jnp.where(upper == 1, af, -1.0)], axis=1).astype(BF16)
    for k in range(KNN):
        edges[k * PTS : (k + 1) * PTS, :] = jnp.where(a2 == jnp.asarray(k, BF16), e2, jnp.zeros_like(e2))
    own_part = lax.dot_general(edge, win[REACH], TN, preferred_element_type=F32)
    nbr = jnp.zeros((HALF, CIN), F32)
    part_cp = {}
    for group in ((0, 1, 2), (6, 7, 8), (3, 4, 5)):
        rows = slice(group[0] * HALF, (group[-1] + 1) * HALF)
        acc[rows, :] = jnp.dot(onehot[rows, :], edges[...], preferred_element_type=F32)
        for w in group:
            ga = acc[w * HALF : (w + 1) * HALF, :].astype(BF16)
            ga = jnp.concatenate([ga[:, :HALF], ga[:, HALF:]], axis=0)
            con = jnp.dot(ga, w_nbr, preferred_element_type=F32)
            if w == REACH:
                con = con + jnp.dot(edge, w_diff, preferred_element_type=F32)
            nbr = nbr + lax.dot_general(ga, win[w], TN, preferred_element_type=F32)
            lo, hi = con[:HALF], con[HALF:]
            mine[w] = jnp.where(c == 0, lo, hi)
            part_out[w] = jnp.where(c == 0, hi, lo).astype(BF16)
            part_cp[w] = rcopy(part_out.at[w], part_in.at[w], pp_s.at[w], pp_r.at[w], partner)
            part_cp[w].start()
    wgv[:, :CIN] = own_part
    wgv[:, CIN:] = nbr - own_part

    a1 = []
    for j, (q, d) in enumerate(zip(plane_at, plane)):
        cp = rcopy(wgv.at[pl.ds(pl.multiple_of(q * 8, 8), 8)], rs_in.at[j], a1s.at[j], a1r.at[j], d)
        cp.start()
        a1.append(cp)

    c_cp = []
    for w in (0, 1, 2, 6, 7, 8, 3, 5):
        part_cp[w].wait_recv()
        summed[w] = (mine[w] + part_in[w].astype(F32)).astype(BF16)
        cp = rcopy(summed.at[w], got.at[8 - w], c_s.at[w], c_r.at[8 - w], (lax.rem(b + w - REACH + NB, NB), c))
        cp.start()
        c_cp.append((w, cp))
    part_cp[REACH].wait_recv()
    total = mine[REACH] + part_in[REACH].astype(F32)

    my_piece = pl.ds(pl.multiple_of(line * 8, 8), 8)
    for cp in a1:
        cp.wait_recv()
    piece[0] = wgv[my_piece, :] + jnp.sum(rs_in[...], axis=0)
    a2c = []
    for j, d in enumerate(zline):
        cp = rcopy(piece.at[0], z_in.at[j], a2s.at[j], a2r.at[j], d)
        cp.start()
        a2c.append(cp)
    for cp in a2c:
        cp.wait_recv()
    piece[1] = (piece[0] + jnp.sum(z_in[...], axis=0)) * (NB * PTS) ** -0.5
    a3c = []
    for j, d in enumerate(plane):
        cp = rcopy(piece.at[1], wgo.at[my_piece], a3s.at[j], a3r.at[j], d)
        cp.start()
        a3c.append(cp)
    wgo[my_piece, :] = piece[1]

    for w, cp in c_cp:
        rcopy(summed.at[w], got.at[w], c_s.at[w], c_r.at[w], partner).wait_recv()
        total = total + got[w].astype(F32)
    fgv[my_rows, :] = total
    fo = rcopy(fgv.at[my_rows], fgv.at[my_rows], fo_s, fo_r, partner)
    fo.start()

    for cp in a3c:
        cp.wait_recv()
    out_wg = pltpu.make_async_copy(wgo, wg_hbm, out_sem.at[0])
    out_wg.start()
    rcopy(fgv.at[my_rows], fgv.at[its_rows], fo_s, fo_r, partner).wait_recv()
    out_fg = pltpu.make_async_copy(fgv, fg_hbm, out_sem.at[1])
    out_fg.start()
    for cp in far_cp + list(half_cp.values()) + list(part_cp.values()) + [cp for _, cp in c_cp] + a1 + a2c + a3c + [fo]:
        cp.wait_send()
    out_wg.wait()
    out_fg.wait()


def on_device(features, out_grad, weight, neighbour_slot, argmax_edge):
    v = pltpu.VMEM
    dma = pltpu.SemaphoreType.DMA
    return pl.pallas_call(
        kernel,
        out_shape=(jax.ShapeDtypeStruct((PTS, CIN), F32), jax.ShapeDtypeStruct((HALF, 2 * CIN), F32)),
        in_specs=[pl.BlockSpec(memory_space=pl.ANY)] * 5,
        out_specs=[pl.BlockSpec(memory_space=pl.ANY)] * 2,
        scratch_shapes=[
            v((SPAN, PTS, CIN), BF16), v((PTS, HALF), BF16), v((HALF, 2 * CIN), BF16), v((PTS, KNN), I32),
            v((PTS, HALF), I32), v((PTS, 128), I32), v((128, PTS), I32), v((HALF, PTS), I32), v((HALF, PTS), I32),
            v((SPAN * HALF, KNN * PTS), BF16), v((KNN * PTS, 2 * HALF), BF16), v((HALF, PTS), F32),
            v((SPAN * HALF, 2 * HALF), F32),
            v((SPAN, HALF, CIN), BF16), v((SPAN, HALF, CIN), BF16), v((SPAN, HALF, CIN), F32),
            v((SPAN, HALF, CIN), BF16), v((SPAN, HALF, CIN), BF16), v((PTS, CIN), F32), v((HALF, 2 * CIN), F32),
            v((15, 8, 2 * CIN), F32), v((7, 8, 2 * CIN), F32), v((2, 8, 2 * CIN), F32), v((HALF, 2 * CIN), F32),
            dma((5,)), dma((SPAN,)), dma((SPAN,)), dma((SPAN,)), dma((SPAN,)), dma((SPAN,)), dma((SPAN,)),
            dma((SPAN,)), dma((SPAN,)), dma((15,)), dma((15,)), dma((7,)), dma((7,)), dma((15,)), dma((15,)),
            dma, dma, dma((2,)),
        ],
        compiler_params=pltpu.CompilerParams(
            collective_id=0, has_side_effects=True, vmem_limit_bytes=56 * 2**20
        ),
        name="edge_backward",
    )(features, out_grad, weight, neighbour_slot, argmax_edge)


def solution(mesh):
    return jax.shard_map(
        on_device,
        mesh=mesh,
        in_specs=(P("blk", None), P("blk", "ch"), P("ch", None), P("blk", None), P("blk", "ch")),
        out_specs=(P("blk", None), P("ch", None)),
        check_vma=False,
    )
```

```python
import jax
import jax.numpy as jnp
from jax import lax
from jax.experimental import pallas as pl
from jax.experimental.pallas import tpu as pltpu
from jax.sharding import PartitionSpec as P

REACH = 4
SPAN = 2 * REACH + 1
NB = 128
PTS = 256
HALF = 128
CIN = 128
KNN = 20
MESH = pl.DeviceIdType.MESH
F32, BF16, I32 = jnp.float32, jnp.bfloat16, jnp.int32
NT = (((1,), (1,)), ((), ()))
TN = (((0,), (0,)), ((), ()))
PAIRS = REACH + 1
SPARE = SPAN


def silu_slope(pre):
    sig = jax.nn.sigmoid(pre)
    return sig * (1.0 + pre * (1.0 - sig))


def kernel(
    f_hbm, g_hbm, w_hbm, s_hbm, a_hbm, fgv, wgo,
    win, gv, wv, sv, av, s_t, low_t, grp_t, onehot, edges, pre, chosen, upper_s, edge_s, nbr,
    con_f, con_b, part_in, summed, got, wgv, rs_in, z_in, piece,
    in_sem, far_s, far_r, half_s, half_r, pp_s, pp_r, c_s, c_r,
    ar_s, ar_r, fo_s, fo_r,
):
    b = lax.axis_index("blk")
    c = lax.axis_index("ch")
    partner = (b, 1 - c)
    line, z = b // 8, b % 8
    x, y = line // 4, line % 4

    def along(k):
        return (lax.rem(b + k + NB, NB), c)

    def in_plane(j):
        t = j + j // 10
        q = lax.rem(x + t // 4 + 2, 4) * 4 + lax.rem(y + t % 4 + 2, 4)
        return q, (q * 8 + z, c)

    def in_line(j):
        return (line * 8 + lax.rem(z + 4 + j + j // 4, 8), c)

    bar = pltpu.get_barrier_semaphore()

    def greet(d):
        pl.semaphore_signal(bar, inc=1, device_id=d, device_id_type=MESH)

    loads = [
        pltpu.make_async_copy(f_hbm, win.at[REACH], in_sem.at[0]),
        pltpu.make_async_copy(s_hbm, sv, in_sem.at[1]),
        pltpu.make_async_copy(a_hbm, av, in_sem.at[2]),
        pltpu.make_async_copy(w_hbm, wv, in_sem.at[3]),
        pltpu.make_async_copy(g_hbm, gv, in_sem.at[4]),
    ]
    loads[0].start()

    @pl.loop(1, REACH + 1)
    def _(k):
        greet(along(k))
        greet(along(-k))

    greet(partner)
    pl.loop(0, 7)(lambda j: greet(in_line(j)))
    pl.loop(0, 15)(lambda j: greet(in_plane(j)[1]))
    for cp in loads[1:]:
        cp.start()
    loads[0].wait()
    pl.semaphore_wait(bar, 2 * REACH + 1 + 7 + 15)

    my_rows = pl.ds(pl.multiple_of(c * HALF, HALF), HALF)
    its_rows = pl.ds(pl.multiple_of((1 - c) * HALF, HALF), HALF)

    def rcopy(src, dst, ss, rs, dev):
        return pltpu.make_async_remote_copy(
            src_ref=src, dst_ref=dst, send_sem=ss, recv_sem=rs, device_id=dev, device_id_type=MESH
        )

    def far_copy(w):
        return rcopy(win.at[REACH, my_rows], win.at[w, my_rows], far_s.at[w], far_r.at[w], along(REACH - w))

    def half_copy(w):
        return rcopy(win.at[w, my_rows], win.at[w, my_rows], half_s.at[w], half_r.at[w], partner)

    def part_copy(w):
        return rcopy(con_b.at[w, its_rows], part_in.at[w], pp_s.at[w], pp_r.at[w], partner)

    def sum_copy(w):
        return rcopy(summed.at[w], got.at[8 - w], c_s.at[w], c_r.at[8 - w], along(w - REACH))

    @pl.loop(1, REACH + 1)
    def _(k):
        far_copy(REACH - k).start()
        far_copy(REACH + k).start()

    for cp in loads[1:]:
        cp.wait()
    s_t[...] = jnp.zeros_like(s_t)
    s_t[:KNN, :] = sv[...]
    idx = jnp.take_along_axis(s_t[...].T, av[...], axis=1, mode="promise_in_bounds")
    idx_t = idx.T
    low_t[...] = idx_t & 127
    grp_t[...] = idx_t >> 7

    def w_nbr():
        return wv[:, CIN:]

    def w_diff():
        return (wv[:, :CIN].astype(F32) - wv[:, CIN:].astype(F32)).astype(BF16)

    ids = [(lax.broadcasted_iota(I32, (16, PTS), 0) + 16 * j).astype(F32).astype(BF16) for j in range(8)]
    one, zero = jnp.ones((16, PTS), BF16), jnp.zeros((16, PTS), BF16)

    @pl.loop(0, KNN)
    def _(k):
        row = s_t[pl.ds(k, 1), :]
        low = (row & 127).astype(F32)
        blk = row >> 8
        cols = pl.ds(pl.multiple_of(k * PTS, PTS), PTS)
        for n in range(2 * PAIRS):
            at = n * HALF
            w = (REACH - n // 2) if n % 2 == 0 else (REACH + n // 2 if n > 1 else SPARE)
            key = jnp.broadcast_to(jnp.where(blk == w, low, -1.0), (16, PTS)).astype(BF16)
            for j in range(8):
                onehot[at + 16 * j : at + 16 * j + 16, cols] = jnp.where(ids[j] == key, one, zero)

    pre[...] = lax.dot_general(w_diff(), win[REACH], NT, preferred_element_type=F32)

    def pick(w):
        vals = lax.dot_general(w_nbr(), win[w], NT, preferred_element_type=F32)
        for h in range(2):
            cols = slice(h * HALF, (h + 1) * HALF)
            low, grp, p = low_t[:, cols], grp_t[:, cols], pre[:, cols]
            for g in range(2):
                table = vals[:, g * HALF : (g + 1) * HALF]
                hit = jnp.take_along_axis(table, low, axis=1, mode="promise_in_bounds")
                p = jnp.where(grp == 2 * w + g, p + hit, p)
            pre[:, cols] = p

    upper_s[...] = (idx >> 7) & 1
    upper = upper_s[...]
    af = av[...].astype(F32)
    chosen[...] = jnp.concatenate(
        [jnp.where(upper == 0, af, -1.0), jnp.where(upper == 1, af, -1.0)], axis=1
    ).astype(BF16)
    nbr[...] = jnp.zeros_like(nbr)
    win[SPARE] = jnp.zeros_like(win[SPARE])

    @pl.loop(0, PAIRS)
    def _(n):
        near, wide = REACH - n, jnp.where(n == 0, SPARE, REACH + n)

        def forward(k):
            for w in (REACH - k, REACH + k):
                far_copy(w).wait_recv()
                half_copy(w).start()

        @pl.when(n < REACH)
        def _():
            forward(n + 1)

        @pl.when(n > 0)
        def _():
            half_copy(near).wait_recv()
            half_copy(wide).wait_recv()

        pick(near)
        pick(wide)
        edge = (gv[...].astype(F32) * silu_slope(pre[...].T)).astype(BF16)
        edge_s[...] = edge
        ef, upper = edge.astype(F32), upper_s[...]
        e2 = jnp.concatenate([jnp.where(upper == 0, ef, 0.0), jnp.where(upper == 1, ef, 0.0)], axis=1).astype(BF16)
        a2 = chosen[...]
        for k in range(KNN):
            edges[k * PTS : (k + 1) * PTS, :] = jnp.where(a2 == jnp.asarray(k, BF16), e2, jnp.zeros_like(e2))
        rows = pl.ds(pl.multiple_of(n * PTS, PTS), PTS)
        sums = jnp.dot(onehot[rows, :], edges[...], preferred_element_type=F32).astype(BF16)
        extra = jnp.zeros((HALF, CIN), F32)
        for m, w in enumerate((near, wide)):
            ga = sums[m * HALF : (m + 1) * HALF, :]
            ga = jnp.concatenate([ga[:, :HALF], ga[:, HALF:]], axis=0)
            extra = extra + lax.dot_general(ga, win[w], TN, preferred_element_type=F32)
            con = jnp.dot(ga, w_nbr(), preferred_element_type=F32)
            con_f[w] = con
            con_b[w] = con.astype(BF16)
        nbr[...] += extra

        @pl.when(n > 0)
        def _():
            part_copy(near).start()
            part_copy(wide).start()

    edge = edge_s[...]
    own_part = lax.dot_general(edge, win[REACH], TN, preferred_element_type=F32)
    wgv[:, :CIN] = own_part
    wgv[:, CIN:] = nbr[...] - own_part

    def rows8(q):
        return pl.ds(pl.multiple_of(q * 8, 8), 8)

    @pl.loop(0, 15)
    def _(j):
        q, d = in_plane(j)
        rcopy(wgv.at[rows8(q)], rs_in.at[j], ar_s.at[0], ar_r.at[0], d).start()

    con = con_f[REACH] + jnp.dot(edge, w_diff(), preferred_element_type=F32)
    con_f[REACH] = con
    con_b[REACH] = con.astype(BF16)
    part_copy(REACH).start()

    def send_on(w):
        part_copy(w).wait_recv()
        summed[w] = (con_f[w, my_rows, :] + part_in[w].astype(F32)).astype(BF16)
        sum_copy(w).start()

    @pl.loop(1, REACH + 1)
    def _(k):
        send_on(REACH - k)
        send_on(REACH + k)

    part_copy(REACH).wait_recv()
    fgv[my_rows, :] = con_f[REACH, my_rows, :] + part_in[REACH].astype(F32)

    my_piece = rows8(line)
    rcopy(rs_in, rs_in, ar_s.at[0], ar_r.at[0], partner).wait_recv()
    piece[0] = wgv[my_piece, :] + jnp.sum(rs_in[...], axis=0)
    pl.loop(0, 7)(lambda j: rcopy(piece.at[0], z_in.at[j], ar_s.at[1], ar_r.at[1], in_line(j)).start())
    rcopy(z_in, z_in, ar_s.at[1], ar_r.at[1], partner).wait_recv()
    piece[1] = (piece[0] + jnp.sum(z_in[...], axis=0)) * (NB * PTS) ** -0.5
    pl.loop(0, 15)(
        lambda j: rcopy(piece.at[1], wgo.at[my_piece], ar_s.at[2], ar_r.at[2], in_plane(j)[1]).start()
    )
    wgo[my_piece, :] = piece[1]

    @pl.loop(1, REACH + 1)
    def _(k):
        for w in (REACH - k, REACH + k):
            rcopy(summed.at[w], got.at[w], c_s.at[w], c_r.at[w], partner).wait_recv()
            fgv[my_rows, :] += got[w].astype(F32)

    fo = rcopy(fgv.at[my_rows], fgv.at[my_rows], fo_s, fo_r, partner)
    fo.start()

    @pl.loop(1, REACH + 1)
    def _(k):
        for w in (REACH - k, REACH + k):
            far_copy(w).wait_send()
            half_copy(w).wait_send()
            part_copy(w).wait_send()
            sum_copy(w).wait_send()

    part_copy(REACH).wait_send()
    rcopy(rs_in, rs_in, ar_s.at[0], ar_r.at[0], partner).wait_send()
    rcopy(z_in, z_in, ar_s.at[1], ar_r.at[1], partner).wait_send()
    rcopy(rs_in, rs_in, ar_s.at[2], ar_r.at[2], partner).wait_send()
    rcopy(rs_in, rs_in, ar_s.at[2], ar_r.at[2], partner).wait_recv()
    rcopy(fgv.at[my_rows], fgv.at[its_rows], fo_s, fo_r, partner).wait()


def flush_kernel(fg_ref, wg_ref, fg_hbm, wg_hbm, sem):
    out_fg = pltpu.make_async_copy(fg_ref, fg_hbm, sem.at[0])
    out_wg = pltpu.make_async_copy(wg_ref, wg_hbm, sem.at[1])
    out_fg.start()
    out_wg.start()
    out_fg.wait()
    out_wg.wait()


def flush(fg, wg):
    return pl.pallas_call(
        flush_kernel,
        out_shape=(jax.ShapeDtypeStruct(fg.shape, F32), jax.ShapeDtypeStruct(wg.shape, F32)),
        in_specs=[pl.BlockSpec(memory_space=pltpu.VMEM)] * 2,
        out_specs=[pl.BlockSpec(memory_space=pl.ANY)] * 2,
        scratch_shapes=[pltpu.SemaphoreType.DMA((2,))],
        name="flush",
    )(pltpu.with_memory_space_constraint(fg, pltpu.VMEM), pltpu.with_memory_space_constraint(wg, pltpu.VMEM))


def on_device(features, out_grad, weight, neighbour_slot, argmax_edge):
    v = pltpu.VMEM
    dma = pltpu.SemaphoreType.DMA
    fg, wg = pl.pallas_call(
        kernel,
        out_shape=(v((PTS, CIN), F32), v((HALF, 2 * CIN), F32)),
        in_specs=[pl.BlockSpec(memory_space=pl.ANY)] * 5,
        out_specs=[pl.BlockSpec(memory_space=pltpu.VMEM)] * 2,
        scratch_shapes=[
            v((SPAN + 1, PTS, CIN), BF16), v((PTS, HALF), BF16), v((HALF, 2 * CIN), BF16), v((KNN, PTS), I32),
            v((PTS, HALF), I32), v((128, PTS), I32), v((HALF, PTS), I32), v((HALF, PTS), I32),
            v((2 * PAIRS * HALF, KNN * PTS), BF16), v((KNN * PTS, 2 * HALF), BF16), v((HALF, PTS), F32),
            v((PTS, 2 * HALF), BF16), v((PTS, HALF), I32), v((PTS, HALF), BF16), v((HALF, CIN), F32),
            v((SPAN + 1, PTS, CIN), F32), v((SPAN + 1, PTS, CIN), BF16), v((SPAN, HALF, CIN), BF16),
            v((SPAN, HALF, CIN), BF16), v((SPAN, HALF, CIN), BF16), v((HALF, 2 * CIN), F32),
            v((15, 8, 2 * CIN), F32), v((7, 8, 2 * CIN), F32), v((2, 8, 2 * CIN), F32),
            dma((5,)), dma((SPAN,)), dma((SPAN,)), dma((SPAN,)), dma((SPAN,)), dma((SPAN,)), dma((SPAN,)),
            dma((SPAN,)), dma((SPAN,)), dma((3,)), dma((3,)),
            dma, dma,
        ],
        compiler_params=pltpu.CompilerParams(
            collective_id=0, has_side_effects=True, vmem_limit_bytes=56 * 2**20
        ),
        name="edge_backward",
    )(features, out_grad, weight, neighbour_slot.T, argmax_edge)
    return flush(fg, wg)


def solution(mesh):
    return jax.shard_map(
        on_device,
        mesh=mesh,
        in_specs=(P("blk", None), P("blk", "ch"), P("ch", None), P("blk", None), P("blk", "ch")),
        out_specs=(P("blk", None), P("ch", None)),
        check_vma=False,
    )
```

```python
import jax
import jax.numpy as jnp
from jax import lax
from jax.experimental import pallas as pl
from jax.experimental.pallas import tpu as pltpu
from jax.sharding import PartitionSpec as P

REACH = 4
SPAN = 2 * REACH + 1
NB = 128
PTS = 256
HALF = 128
CIN = 128
KNN = 20
MESH = pl.DeviceIdType.MESH
F32, BF16, I32 = jnp.float32, jnp.bfloat16, jnp.int32
NT = (((1,), (1,)), ((), ()))
TN = (((0,), (0,)), ((), ()))
PAIRS = REACH + 1
SPARE = SPAN


def silu_slope(pre):
    sig = jax.nn.sigmoid(pre)
    return sig * (1.0 + pre * (1.0 - sig))


def kernel(
    f_hbm, g_hbm, w_hbm, s_hbm, a_hbm, fgv, wgo,
    win, gv, wv, sv, av, s_t, low_t, grp_t, onehot, edges, pre, chosen, upper_s, edge_s, nbr,
    con_f, con_b, part_in, summed, got, wgv, wgb, wg_all, rs_in, z_in, piece_b,
    in_sem, far_s, far_r, half_s, half_r, pp_s, pp_r, c_s, c_r,
    ar_s, ar_r, fo_s, fo_r,
):
    b = lax.axis_index("blk")
    c = lax.axis_index("ch")
    partner = (b, 1 - c)
    line, z = b // 8, b % 8
    x, y = line // 4, line % 4

    def along(k):
        return (lax.rem(b + k + NB, NB), c)

    xs = [lax.rem(x + d, 4) * 32 for d in (2, 1, 3)] + [x * 32]
    ys = [lax.rem(y + d, 4) * 8 for d in (2, 1, 3)] + [y * 8]
    at_plane = [(p, r) for t in range(6) for p in range(4) for r in range(4) if p + r == t]
    plane = [xs[p] + ys[r] for p, r in at_plane]
    across = [(q + z, c) for q in plane]
    zline = [(line * 8 + lax.rem(z + d, 8), c) for d in (4, 3, 5, 2, 6, 1, 7)]

    bar = pltpu.get_barrier_semaphore()

    def greet(d):
        pl.semaphore_signal(bar, inc=1, device_id=d, device_id_type=MESH)

    loads = [
        pltpu.make_async_copy(f_hbm, win.at[REACH], in_sem.at[0]),
        pltpu.make_async_copy(s_hbm, sv, in_sem.at[1]),
        pltpu.make_async_copy(a_hbm, av, in_sem.at[2]),
        pltpu.make_async_copy(w_hbm, wv, in_sem.at[3]),
        pltpu.make_async_copy(g_hbm, gv, in_sem.at[4]),
    ]
    loads[0].start()

    for k in (4, 3, 2, 1):
        greet(along(k))
        greet(along(-k))
    for d in across + zline + [partner]:
        greet(d)
    for cp in loads[1:]:
        cp.start()
    loads[0].wait()
    pl.semaphore_wait(bar, 2 * REACH + 1 + 7 + 15)

    my_rows = pl.ds(pl.multiple_of(c * HALF, HALF), HALF)
    its_rows = pl.ds(pl.multiple_of((1 - c) * HALF, HALF), HALF)

    def rcopy(src, dst, ss, rs, dev):
        return pltpu.make_async_remote_copy(
            src_ref=src, dst_ref=dst, send_sem=ss, recv_sem=rs, device_id=dev, device_id_type=MESH
        )

    def far_copy(w):
        return rcopy(win.at[REACH, my_rows], win.at[w, my_rows], far_s.at[w], far_r.at[w], along(REACH - w))

    def half_copy(w):
        return rcopy(win.at[w, my_rows], win.at[w, my_rows], half_s.at[w], half_r.at[w], partner)

    def part_copy(w):
        return rcopy(con_b.at[w, its_rows], part_in.at[w], pp_s.at[w], pp_r.at[w], partner)

    def sum_copy(w):
        return rcopy(summed.at[w], got.at[8 - w], c_s.at[w], c_r.at[8 - w], along(w - REACH))

    @pl.loop(1, REACH + 1)
    def _(k):
        far_copy(REACH - k).start()
        far_copy(REACH + k).start()

    for cp in loads[1:]:
        cp.wait()
    s_t[...] = jnp.zeros_like(s_t)
    s_t[:KNN, :] = sv[...]
    idx = jnp.take_along_axis(s_t[...].T, av[...], axis=1, mode="promise_in_bounds")
    idx_t = idx.T
    low_t[...] = idx_t & 127
    grp_t[...] = idx_t >> 7

    def w_nbr():
        return wv[:, CIN:]

    def w_diff():
        return (wv[:, :CIN].astype(F32) - wv[:, CIN:].astype(F32)).astype(BF16)

    ids = [(lax.broadcasted_iota(I32, (16, PTS), 0) + 16 * j).astype(F32).astype(BF16) for j in range(8)]
    one, zero = jnp.ones((16, PTS), BF16), jnp.zeros((16, PTS), BF16)

    @pl.loop(0, KNN)
    def _(k):
        row = s_t[pl.ds(k, 1), :]
        low = (row & 127).astype(F32)
        blk = row >> 8
        cols = pl.ds(pl.multiple_of(k * PTS, PTS), PTS)
        for n in range(2 * PAIRS):
            at = n * HALF
            w = (REACH - n // 2) if n % 2 == 0 else (REACH + n // 2 if n > 1 else SPARE)
            key = jnp.broadcast_to(jnp.where(blk == w, low, -1.0), (16, PTS)).astype(BF16)
            for j in range(8):
                onehot[at + 16 * j : at + 16 * j + 16, cols] = jnp.where(ids[j] == key, one, zero)

    pre[...] = lax.dot_general(w_diff(), win[REACH], NT, preferred_element_type=F32)

    def pick(w):
        vals = lax.dot_general(w_nbr(), win[w], NT, preferred_element_type=F32)
        for h in range(2):
            cols = slice(h * HALF, (h + 1) * HALF)
            low, grp, p = low_t[:, cols], grp_t[:, cols], pre[:, cols]
            for g in range(2):
                table = vals[:, g * HALF : (g + 1) * HALF]
                hit = jnp.take_along_axis(table, low, axis=1, mode="promise_in_bounds")
                p = jnp.where(grp == 2 * w + g, p + hit, p)
            pre[:, cols] = p

    upper_s[...] = (idx >> 7) & 1
    upper = upper_s[...]
    af = av[...].astype(F32)
    chosen[...] = jnp.concatenate(
        [jnp.where(upper == 0, af, -1.0), jnp.where(upper == 1, af, -1.0)], axis=1
    ).astype(BF16)
    nbr[...] = jnp.zeros_like(nbr)
    win[SPARE] = jnp.zeros_like(win[SPARE])

    def send_on(k):
        for w in (REACH - k, REACH + k):
            part_copy(w).wait_recv()
            summed[w] = (con_f[w, my_rows, :] + part_in[w].astype(F32)).astype(BF16)
            sum_copy(w).start()

    @pl.loop(0, PAIRS)
    def _(n):
        near, wide = REACH - n, jnp.where(n == 0, SPARE, REACH + n)

        def forward(k):
            for w in (REACH - k, REACH + k):
                far_copy(w).wait_recv()
                half_copy(w).start()

        @pl.when(n < REACH - 1)
        def _():
            forward(n + 1)

        @pl.when(n > 0)
        def _():
            half_copy(near).wait_recv()
            half_copy(wide).wait_recv()

        pick(near)
        pick(wide)
        edge = (gv[...].astype(F32) * silu_slope(pre[...].T)).astype(BF16)
        edge_s[...] = edge
        ef, upper = edge.astype(F32), upper_s[...]
        e2 = jnp.concatenate([jnp.where(upper == 0, ef, 0.0), jnp.where(upper == 1, ef, 0.0)], axis=1).astype(BF16)
        a2 = chosen[...]
        for k in range(KNN):
            edges[k * PTS : (k + 1) * PTS, :] = jnp.where(a2 == jnp.asarray(k, BF16), e2, jnp.zeros_like(e2))
        rows = pl.ds(pl.multiple_of(n * PTS, PTS), PTS)
        sums = jnp.dot(onehot[rows, :], edges[...], preferred_element_type=F32).astype(BF16)
        extra = jnp.zeros((HALF, CIN), F32)
        for m, w in enumerate((near, wide)):
            ga = sums[m * HALF : (m + 1) * HALF, :]
            ga = jnp.concatenate([ga[:, :HALF], ga[:, HALF:]], axis=0)
            extra = extra + lax.dot_general(ga, win[w], TN, preferred_element_type=F32)
            con = jnp.dot(ga, w_nbr(), preferred_element_type=F32)
            con_f[w] = con
            con_b[w] = con.astype(BF16)
        nbr[...] += extra

        @pl.when(n > 0)
        def _():
            part_copy(near).start()
            part_copy(wide).start()

        @pl.when(n == REACH - 1)
        def _():
            forward(REACH)
            pl.loop(1, REACH)(send_on)

    edge = edge_s[...]
    own_part = lax.dot_general(edge, win[REACH], TN, preferred_element_type=F32)
    both = (own_part, nbr[...] - own_part)
    for q in range(16):
        wgv[q] = jnp.concatenate([v[q * 8 : q * 8 + 8, :] for v in both], axis=0)
    wgb[...] = wgv[...].astype(BF16)

    for j, (q, d) in enumerate(zip(plane, across)):
        rcopy(wgb.at[q // 8], rs_in.at[j], ar_s.at[0], ar_r.at[0], d).start()

    con = con_f[REACH] + jnp.dot(edge, w_diff(), preferred_element_type=F32)
    con_f[REACH] = con
    con_b[REACH] = con.astype(BF16)
    part_copy(REACH).start()

    send_on(REACH)
    part_copy(REACH).wait_recv()
    fgv[my_rows, :] = con_f[REACH, my_rows, :] + part_in[REACH].astype(F32)

    rcopy(rs_in, rs_in, ar_s.at[0], ar_r.at[0], partner).wait_recv()
    piece = wgv[line] + jnp.sum(rs_in[...].astype(F32), axis=0)
    piece_b[0] = piece.astype(BF16)
    for j, d in enumerate(zline):
        rcopy(piece_b.at[0], z_in.at[j], ar_s.at[1], ar_r.at[1], d).start()
    rcopy(z_in, z_in, ar_s.at[1], ar_r.at[1], partner).wait_recv()
    piece = (piece + jnp.sum(z_in[...].astype(F32), axis=0)) * (NB * PTS) ** -0.5
    piece_b[1] = piece.astype(BF16)
    for d in across:
        rcopy(piece_b.at[1], wg_all.at[line], ar_s.at[2], ar_r.at[2], d).start()
    wg_all[line] = piece_b[1]

    @pl.loop(1, REACH + 1)
    def _(k):
        for w in (REACH - k, REACH + k):
            rcopy(summed.at[w], got.at[w], c_s.at[w], c_r.at[w], partner).wait_recv()
            fgv[my_rows, :] += got[w].astype(F32)

    fo = rcopy(fgv.at[my_rows], fgv.at[my_rows], fo_s, fo_r, partner)
    fo.start()

    @pl.loop(1, REACH + 1)
    def _(k):
        for w in (REACH - k, REACH + k):
            far_copy(w).wait_send()
            half_copy(w).wait_send()
            part_copy(w).wait_send()
            sum_copy(w).wait_send()

    part_copy(REACH).wait_send()
    rcopy(rs_in, rs_in, ar_s.at[0], ar_r.at[0], partner).wait_send()
    rcopy(z_in, z_in, ar_s.at[1], ar_r.at[1], partner).wait_send()
    rcopy(rs_in, rs_in, ar_s.at[2], ar_r.at[2], partner).wait_send()
    rcopy(rs_in, rs_in, ar_s.at[2], ar_r.at[2], partner).wait_recv()
    for q in range(16):
        whole = wg_all[q].astype(F32)
        wgo[q * 8 : q * 8 + 8, :CIN] = whole[:8]
        wgo[q * 8 : q * 8 + 8, CIN:] = whole[8:]
    rcopy(fgv.at[my_rows], fgv.at[its_rows], fo_s, fo_r, partner).wait()


def flush_kernel(fg_ref, wg_ref, fg_hbm, wg_hbm, sem):
    out_fg = pltpu.make_async_copy(fg_ref, fg_hbm, sem.at[0])
    out_wg = pltpu.make_async_copy(wg_ref, wg_hbm, sem.at[1])
    out_fg.start()
    out_wg.start()
    out_fg.wait()
    out_wg.wait()


def flush(fg, wg):
    return pl.pallas_call(
        flush_kernel,
        out_shape=(jax.ShapeDtypeStruct(fg.shape, F32), jax.ShapeDtypeStruct(wg.shape, F32)),
        in_specs=[pl.BlockSpec(memory_space=pltpu.VMEM)] * 2,
        out_specs=[pl.BlockSpec(memory_space=pl.ANY)] * 2,
        scratch_shapes=[pltpu.SemaphoreType.DMA((2,))],
        name="flush",
    )(pltpu.with_memory_space_constraint(fg, pltpu.VMEM), pltpu.with_memory_space_constraint(wg, pltpu.VMEM))


def on_device(features, out_grad, weight, neighbour_slot, argmax_edge):
    v = pltpu.VMEM
    dma = pltpu.SemaphoreType.DMA
    fg, wg = pl.pallas_call(
        kernel,
        out_shape=(v((PTS, CIN), F32), v((HALF, 2 * CIN), F32)),
        in_specs=[pl.BlockSpec(memory_space=pl.ANY)] * 5,
        out_specs=[pl.BlockSpec(memory_space=pltpu.VMEM)] * 2,
        scratch_shapes=[
            v((SPAN + 1, PTS, CIN), BF16), v((PTS, HALF), BF16), v((HALF, 2 * CIN), BF16), v((KNN, PTS), I32),
            v((PTS, HALF), I32), v((128, PTS), I32), v((HALF, PTS), I32), v((HALF, PTS), I32),
            v((2 * PAIRS * HALF, KNN * PTS), BF16), v((KNN * PTS, 2 * HALF), BF16), v((HALF, PTS), F32),
            v((PTS, 2 * HALF), BF16), v((PTS, HALF), I32), v((PTS, HALF), BF16), v((HALF, CIN), F32),
            v((SPAN + 1, PTS, CIN), F32), v((SPAN + 1, PTS, CIN), BF16), v((SPAN, HALF, CIN), BF16),
            v((SPAN, HALF, CIN), BF16), v((SPAN, HALF, CIN), BF16), v((16, 16, CIN), F32),
            v((16, 16, CIN), BF16), v((16, 16, CIN), BF16),
            v((15, 16, CIN), BF16), v((7, 16, CIN), BF16), v((2, 16, CIN), BF16),
            dma((5,)), dma((SPAN,)), dma((SPAN,)), dma((SPAN,)), dma((SPAN,)), dma((SPAN,)), dma((SPAN,)),
            dma((SPAN,)), dma((SPAN,)), dma((3,)), dma((3,)),
            dma, dma,
        ],
        compiler_params=pltpu.CompilerParams(
            collective_id=0, has_side_effects=True, vmem_limit_bytes=56 * 2**20
        ),
        name="edge_backward",
    )(features, out_grad, weight, neighbour_slot.T, argmax_edge)
    return flush(fg, wg)


def solution(mesh):
    return jax.shard_map(
        on_device,
        mesh=mesh,
        in_specs=(P("blk", None), P("blk", "ch"), P("ch", None), P("blk", None), P("blk", "ch")),
        out_specs=(P("blk", None), P("ch", None)),
        check_vma=False,
    )
```

```python
import jax
import jax.numpy as jnp
from jax import lax
from jax.experimental import pallas as pl
from jax.experimental.pallas import tpu as pltpu
from jax.sharding import PartitionSpec as P

REACH = 4
SPAN = 2 * REACH + 1
NB = 128
PTS = 256
HALF = 128
CIN = 128
KNN = 20
MESH = pl.DeviceIdType.MESH
F32, BF16, I32 = jnp.float32, jnp.bfloat16, jnp.int32
NT = (((1,), (1,)), ((), ()))
TN = (((0,), (0,)), ((), ()))
PAIRS = REACH + 1
SPARE = SPAN


def silu_slope(pre):
    sig = jax.nn.sigmoid(pre)
    return sig * (1.0 + pre * (1.0 - sig))


def kernel(
    f_hbm, g_hbm, w_hbm, s_hbm, a_hbm, fgv, wgo,
    win, gv, wv, sv, av, s_t, low_t, grp_t, onehot, edges, pre, chosen, upper_s, edge_s, nbr,
    con_f, con_b, part_in, summed, got, wgv, wgb, wg_all, rs_in, z_in, piece_b,
    in_sem, far_s, far_r, half_s, half_r, pp_s, pp_r, c_s, c_r,
    ar_s, ar_r, fo_s, fo_r,
):
    b = lax.axis_index("blk")
    c = lax.axis_index("ch")
    partner = (b, 1 - c)
    line, z = b // 8, b % 8
    x, y = line // 4, line % 4

    def along(k):
        return (lax.rem(b + k + NB, NB), c)

    xs = [lax.rem(x + d, 4) * 32 for d in (2, 1, 3)] + [x * 32]
    ys = [lax.rem(y + d, 4) * 8 for d in (2, 1, 3)] + [y * 8]
    at_plane = [(p, r) for t in range(6) for p in range(4) for r in range(4) if p + r == t]
    plane = [xs[p] + ys[r] for p, r in at_plane]
    across = [(q + z, c) for q in plane]
    zline = [(line * 8 + lax.rem(z + d, 8), c) for d in (4, 3, 5, 2, 6, 1, 7)]

    bar = pltpu.get_barrier_semaphore()

    def greet(d):
        pl.semaphore_signal(bar, inc=1, device_id=d, device_id_type=MESH)

    loads = [
        pltpu.make_async_copy(f_hbm, win.at[REACH], in_sem.at[0]),
        pltpu.make_async_copy(s_hbm, sv, in_sem.at[1]),
        pltpu.make_async_copy(a_hbm, av, in_sem.at[2]),
        pltpu.make_async_copy(w_hbm, wv, in_sem.at[3]),
        pltpu.make_async_copy(g_hbm, gv, in_sem.at[4]),
    ]
    loads[0].start()

    for k in (4, 3, 2, 1):
        greet(along(k))
        greet(along(-k))
    for d in across + zline + [partner]:
        greet(d)
    for cp in loads[1:]:
        cp.start()
    loads[0].wait()
    pl.semaphore_wait(bar, 2 * REACH + 1 + 7 + 15)

    my_rows = pl.ds(pl.multiple_of(c * HALF, HALF), HALF)
    its_rows = pl.ds(pl.multiple_of((1 - c) * HALF, HALF), HALF)

    def rcopy(src, dst, ss, rs, dev):
        return pltpu.make_async_remote_copy(
            src_ref=src, dst_ref=dst, send_sem=ss, recv_sem=rs, device_id=dev, device_id_type=MESH
        )

    side = 1 - 2 * c

    def far_copy(k):
        w = REACH - side * k
        return rcopy(win.at[REACH], win.at[w], far_s.at[k], far_r.at[k], along(side * k))

    def swap_copy(k):
        w = REACH - side * k
        return rcopy(win.at[w], win.at[w], half_s.at[k], half_r.at[k], partner)

    def part_copy(w):
        return rcopy(con_b.at[w, its_rows], part_in.at[w], pp_s.at[w], pp_r.at[w], partner)

    def sum_copy(w):
        return rcopy(summed.at[w], got.at[8 - w], c_s.at[w], c_r.at[8 - w], along(w - REACH))

    @pl.loop(1, REACH + 1)
    def _(k):
        far_copy(k).start()

    for cp in loads[1:]:
        cp.wait()
    s_t[...] = jnp.zeros_like(s_t)
    s_t[:KNN, :] = sv[...]
    idx = jnp.take_along_axis(s_t[...].T, av[...], axis=1, mode="promise_in_bounds")
    idx_t = idx.T
    low_t[...] = idx_t & 127
    grp_t[...] = idx_t >> 7

    def w_nbr():
        return wv[:, CIN:]

    def w_diff():
        return (wv[:, :CIN].astype(F32) - wv[:, CIN:].astype(F32)).astype(BF16)

    ids = [(lax.broadcasted_iota(I32, (16, PTS), 0) + 16 * j).astype(F32).astype(BF16) for j in range(8)]
    one, zero = jnp.ones((16, PTS), BF16), jnp.zeros((16, PTS), BF16)

    @pl.loop(0, KNN)
    def _(k):
        row = s_t[pl.ds(k, 1), :]
        low = (row & 127).astype(F32)
        blk = row >> 8
        cols = pl.ds(pl.multiple_of(k * PTS, PTS), PTS)
        for n in range(2 * PAIRS):
            at = n * HALF
            w = (REACH - n // 2) if n % 2 == 0 else (REACH + n // 2 if n > 1 else SPARE)
            key = jnp.broadcast_to(jnp.where(blk == w, low, -1.0), (16, PTS)).astype(BF16)
            for j in range(8):
                onehot[at + 16 * j : at + 16 * j + 16, cols] = jnp.where(ids[j] == key, one, zero)

    pre[...] = lax.dot_general(w_diff(), win[REACH], NT, preferred_element_type=F32)

    def pick(w):
        vals = lax.dot_general(w_nbr(), win[w], NT, preferred_element_type=F32)
        for h in range(2):
            cols = slice(h * HALF, (h + 1) * HALF)
            low, grp, p = low_t[:, cols], grp_t[:, cols], pre[:, cols]
            for g in range(2):
                table = vals[:, g * HALF : (g + 1) * HALF]
                hit = jnp.take_along_axis(table, low, axis=1, mode="promise_in_bounds")
                p = jnp.where(grp == 2 * w + g, p + hit, p)
            pre[:, cols] = p

    upper_s[...] = (idx >> 7) & 1
    upper = upper_s[...]
    af = av[...].astype(F32)
    chosen[...] = jnp.concatenate(
        [jnp.where(upper == 0, af, -1.0), jnp.where(upper == 1, af, -1.0)], axis=1
    ).astype(BF16)
    nbr[...] = jnp.zeros_like(nbr)
    win[SPARE] = jnp.zeros_like(win[SPARE])

    def send_on(k):
        for w in (REACH - k, REACH + k):
            part_copy(w).wait_recv()
            summed[w] = (con_f[w, my_rows, :] + part_in[w].astype(F32)).astype(BF16)
            sum_copy(w).start()

    @pl.loop(0, PAIRS)
    def _(n):
        near, wide = REACH - n, jnp.where(n == 0, SPARE, REACH + n)

        def forward(k):
            far_copy(k).wait_recv()
            swap_copy(k).start()

        @pl.when(n < REACH - 1)
        def _():
            forward(n + 1)

        @pl.when(n > 0)
        def _():
            swap_copy(n).wait_recv()

        pick(near)
        pick(wide)
        edge = (gv[...].astype(F32) * silu_slope(pre[...].T)).astype(BF16)
        edge_s[...] = edge
        ef, upper = edge.astype(F32), upper_s[...]
        e2 = jnp.concatenate([jnp.where(upper == 0, ef, 0.0), jnp.where(upper == 1, ef, 0.0)], axis=1).astype(BF16)
        a2 = chosen[...]
        for k in range(KNN):
            edges[k * PTS : (k + 1) * PTS, :] = jnp.where(a2 == jnp.asarray(k, BF16), e2, jnp.zeros_like(e2))
        rows = pl.ds(pl.multiple_of(n * PTS, PTS), PTS)
        sums = jnp.dot(onehot[rows, :], edges[...], preferred_element_type=F32).astype(BF16)
        extra = jnp.zeros((HALF, CIN), F32)
        for m, w in enumerate((near, wide)):
            ga = sums[m * HALF : (m + 1) * HALF, :]
            ga = jnp.concatenate([ga[:, :HALF], ga[:, HALF:]], axis=0)
            extra = extra + lax.dot_general(ga, win[w], TN, preferred_element_type=F32)
            con = jnp.dot(ga, w_nbr(), preferred_element_type=F32)
            con_f[w] = con
            con_b[w] = con.astype(BF16)
        nbr[...] += extra

        @pl.when(n > 0)
        def _():
            part_copy(near).start()
            part_copy(wide).start()

        @pl.when(n == REACH - 1)
        def _():
            forward(REACH)
            pl.loop(1, REACH)(send_on)

    edge = edge_s[...]
    own_part = lax.dot_general(edge, win[REACH], TN, preferred_element_type=F32)
    both = (own_part, nbr[...] - own_part)
    for q in range(16):
        wgv[q] = jnp.concatenate([v[q * 8 : q * 8 + 8, :] for v in both], axis=0)
    wgb[...] = wgv[...].astype(BF16)

    for j, (q, d) in enumerate(zip(plane, across)):
        rcopy(wgb.at[q // 8], rs_in.at[j], ar_s.at[0], ar_r.at[0], d).start()

    con = con_f[REACH] + jnp.dot(edge, w_diff(), preferred_element_type=F32)
    con_f[REACH] = con
    con_b[REACH] = con.astype(BF16)
    part_copy(REACH).start()

    send_on(REACH)
    part_copy(REACH).wait_recv()
    fgv[my_rows, :] = con_f[REACH, my_rows, :] + part_in[REACH].astype(F32)

    rcopy(rs_in, rs_in, ar_s.at[0], ar_r.at[0], partner).wait_recv()
    piece = wgv[line] + jnp.sum(rs_in[...].astype(F32), axis=0)
    piece_b[0] = piece.astype(BF16)
    for j, d in enumerate(zline):
        rcopy(piece_b.at[0], z_in.at[j], ar_s.at[1], ar_r.at[1], d).start()
    rcopy(z_in, z_in, ar_s.at[1], ar_r.at[1], partner).wait_recv()
    piece = (piece + jnp.sum(z_in[...].astype(F32), axis=0)) * (NB * PTS) ** -0.5
    piece_b[1] = piece.astype(BF16)
    for d in across:
        rcopy(piece_b.at[1], wg_all.at[line], ar_s.at[2], ar_r.at[2], d).start()
    wg_all[line] = piece_b[1]

    @pl.loop(1, REACH + 1)
    def _(k):
        for w in (REACH - k, REACH + k):
            rcopy(summed.at[w], got.at[w], c_s.at[w], c_r.at[w], partner).wait_recv()
            fgv[my_rows, :] += got[w].astype(F32)

    fo = rcopy(fgv.at[my_rows], fgv.at[my_rows], fo_s, fo_r, partner)
    fo.start()

    @pl.loop(1, REACH + 1)
    def _(k):
        for w in (REACH - k, REACH + k):
            part_copy(w).wait_send()
            sum_copy(w).wait_send()
        far_copy(k).wait_send()
        swap_copy(k).wait_send()

    part_copy(REACH).wait_send()
    rcopy(rs_in, rs_in, ar_s.at[0], ar_r.at[0], partner).wait_send()
    rcopy(z_in, z_in, ar_s.at[1], ar_r.at[1], partner).wait_send()
    rcopy(rs_in, rs_in, ar_s.at[2], ar_r.at[2], partner).wait_send()
    rcopy(rs_in, rs_in, ar_s.at[2], ar_r.at[2], partner).wait_recv()
    for q in range(16):
        whole = wg_all[q].astype(F32)
        wgo[q * 8 : q * 8 + 8, :CIN] = whole[:8]
        wgo[q * 8 : q * 8 + 8, CIN:] = whole[8:]
    rcopy(fgv.at[my_rows], fgv.at[its_rows], fo_s, fo_r, partner).wait()


def flush_kernel(fg_ref, wg_ref, fg_hbm, wg_hbm, sem):
    out_fg = pltpu.make_async_copy(fg_ref, fg_hbm, sem.at[0])
    out_wg = pltpu.make_async_copy(wg_ref, wg_hbm, sem.at[1])
    out_fg.start()
    out_wg.start()
    out_fg.wait()
    out_wg.wait()


def flush(fg, wg):
    return pl.pallas_call(
        flush_kernel,
        out_shape=(jax.ShapeDtypeStruct(fg.shape, F32), jax.ShapeDtypeStruct(wg.shape, F32)),
        in_specs=[pl.BlockSpec(memory_space=pltpu.VMEM)] * 2,
        out_specs=[pl.BlockSpec(memory_space=pl.ANY)] * 2,
        scratch_shapes=[pltpu.SemaphoreType.DMA((2,))],
        name="flush",
    )(pltpu.with_memory_space_constraint(fg, pltpu.VMEM), pltpu.with_memory_space_constraint(wg, pltpu.VMEM))


def on_device(features, out_grad, weight, neighbour_slot, argmax_edge):
    v = pltpu.VMEM
    dma = pltpu.SemaphoreType.DMA
    fg, wg = pl.pallas_call(
        kernel,
        out_shape=(v((PTS, CIN), F32), v((HALF, 2 * CIN), F32)),
        in_specs=[pl.BlockSpec(memory_space=pl.ANY)] * 5,
        out_specs=[pl.BlockSpec(memory_space=pltpu.VMEM)] * 2,
        scratch_shapes=[
            v((SPAN + 1, PTS, CIN), BF16), v((PTS, HALF), BF16), v((HALF, 2 * CIN), BF16), v((KNN, PTS), I32),
            v((PTS, HALF), I32), v((128, PTS), I32), v((HALF, PTS), I32), v((HALF, PTS), I32),
            v((2 * PAIRS * HALF, KNN * PTS), BF16), v((KNN * PTS, 2 * HALF), BF16), v((HALF, PTS), F32),
            v((PTS, 2 * HALF), BF16), v((PTS, HALF), I32), v((PTS, HALF), BF16), v((HALF, CIN), F32),
            v((SPAN + 1, PTS, CIN), F32), v((SPAN + 1, PTS, CIN), BF16), v((SPAN, HALF, CIN), BF16),
            v((SPAN, HALF, CIN), BF16), v((SPAN, HALF, CIN), BF16), v((16, 16, CIN), F32),
            v((16, 16, CIN), BF16), v((16, 16, CIN), BF16),
            v((15, 16, CIN), BF16), v((7, 16, CIN), BF16), v((2, 16, CIN), BF16),
            dma((5,)), dma((SPAN,)), dma((SPAN,)), dma((SPAN,)), dma((SPAN,)), dma((SPAN,)), dma((SPAN,)),
            dma((SPAN,)), dma((SPAN,)), dma((3,)), dma((3,)),
            dma, dma,
        ],
        compiler_params=pltpu.CompilerParams(
            collective_id=0, has_side_effects=True, vmem_limit_bytes=56 * 2**20
        ),
        name="edge_backward",
    )(features, out_grad, weight, neighbour_slot.T, argmax_edge)
    return flush(fg, wg)


def solution(mesh):
    return jax.shard_map(
        on_device,
        mesh=mesh,
        in_specs=(P("blk", None), P("blk", "ch"), P("ch", None), P("blk", None), P("blk", "ch")),
        out_specs=(P("blk", None), P("ch", None)),
        check_vma=False,
    )
```
